32 devices in a mesh: px: 4 (over x, core), py: 8 (over z, y).
Axes of the slice: x: 2, y: 2, z: 4, core: 2. Of those that a mesh axis runs over, the one named last changes fastest.
Arguments:
- root_density: float32 [384, 384, 384], P('px', 'py'), may hold values from -6 to 6
- subgrid_density: float32 [256, 32, 1024], P(('px', 'py')), may hold values from -24 to 24
- velocity: float32 [3, 256, 32, 1024], P(None, ('px', 'py')), may hold values from -6 to 6
- slot_anchor: int32 [3, 256], replicated, may hold values from 0 to 376, as said below
- slot_count: int32 [32], replicated, may hold values from 1 to 8, as said below
- neighbour: int32 [2, 256], replicated, may hold values from -1 to 255, as said below
Outputs:
- coarse_potential: float32 [384, 384, 384], P('px', 'py')
- subgrid_potential: float32 [256, 32, 1024], P(('px', 'py'))
- kicked_velocity: float32 [3, 256, 32, 1024], P(None, ('px', 'py'))
The draws below stay inside these ranges and needn't reach their ends.
Inputs may be any that keep to these rules, and one draw needn't show every extreme that they name: Slot j of device d is slot d * 8 + j, devices numbered in the order of px+py; it is live when j < slot_count[d]. Some device has every slot live. `slot_anchor`: entries are multiples of 8; live slots cover distinct regions of 8^3 root cells; empty slots hold 0. The region of live slot j of the device at px = p, py = q has its lower corner among the root cells that the device at px = p, py = (q + j) mod 8 holds of root_density. neighbour[0, s] is s - 8 or -1 and neighbour[1, s] is s + 8 or -1, the same slot of the device one index lower or higher along py with the same px; where set, both slots are live and the two regions lie next to each other along the second dimension, the lower one below. Empty slots hold -1.
All inputs are finite; a program needn't handle non-finite values.
Results may differ from the reference program's by a relative error of at most 0.000094.
Values sent between devices are 32-bit elements; how exact they have to be, the bound alone decides.
A program may use at most 192 MiB of HBM per device.

```python
import jax
import jax.numpy as jnp
from jax import lax

NR = 384
REG = 8
REF = 4
SWEEPS = 4
SUBGRID_CELLS = 32
DEVICE_SLOTS = 8
TOTAL_SLOTS = 256
DEVICES = 32


def slot_layout(key):
    base_key = jax.random.fold_in(key, 4021)
    count_key, busy_key, place_key, shift_random_key, border_key, face_side_key = jax.random.split(base_key, 6)
    rows_px = DEVICES // DEVICE_SLOTS
    wave_band = NR // DEVICE_SLOTS // REG
    first_band = NR // rows_px // REG
    third_band = NR // REG
    counts = jax.random.randint(count_key, (DEVICES,), 1, DEVICE_SLOTS + 1, dtype=jnp.int32)
    busiest = jax.random.permutation(busy_key, DEVICES)[:2]
    counts = counts.at[busiest].set(DEVICE_SLOTS)
    row_keys = jax.random.split(place_key, rows_px)
    picks = jax.vmap(lambda row_key: jax.random.permutation(row_key, first_band * third_band)[:DEVICE_SLOTS])(row_keys)
    picks = picks.astype(jnp.int32)
    slot_numbers = jnp.arange(TOTAL_SLOTS, dtype=jnp.int32)
    owners = slot_numbers // DEVICE_SLOTS
    within = slot_numbers % DEVICE_SLOTS
    row_place = owners // DEVICE_SLOTS
    column_place = owners % DEVICE_SLOTS
    live_mask = within < counts[owners]
    pair = picks[row_place, within]
    first = row_place * first_band + pair // third_band
    third = pair % third_band
    source_column = (column_place + within) % DEVICE_SLOTS
    constant_shift = jax.random.randint(shift_random_key, (TOTAL_SLOTS,), 0, wave_band, dtype=jnp.int32)
    border_face = jax.random.randint(border_key, (TOTAL_SLOTS,), 0, 2, dtype=jnp.int32)
    face_side = jax.random.randint(face_side_key, (TOTAL_SLOTS,), 0, 2, dtype=jnp.int32)
    offset = jnp.where(border_face == 1, face_side * (wave_band - 1), constant_shift)
    second = source_column * wave_band + offset
    anchor = jnp.stack([first * REG, second * REG, third * REG]).astype(jnp.int32)
    anchor = jnp.where(live_mask[None, :], anchor, 0)
    upper_neighbour_slot = jnp.minimum(slot_numbers + DEVICE_SLOTS, TOTAL_SLOTS - 1)
    has_upper = live_mask & (column_place < DEVICE_SLOTS - 1) & live_mask[upper_neighbour_slot] & (offset == wave_band - 1) & (offset[upper_neighbour_slot] == 0) & (source_column < DEVICE_SLOTS - 1)
    lower_id = jnp.maximum(slot_numbers - DEVICE_SLOTS, 0)
    has_lower = live_mask & (column_place > 0) & live_mask[lower_id] & (offset[lower_id] == wave_band - 1) & (offset == 0) & (source_column[lower_id] < DEVICE_SLOTS - 1)
    upper_slot = jnp.where(has_upper, slot_numbers + DEVICE_SLOTS, -1)
    lower_slot = jnp.where(has_lower, slot_numbers - DEVICE_SLOTS, -1)
    return (anchor, counts.astype(jnp.int32), jnp.stack([lower_slot, upper_slot]).astype(jnp.int32))


def draw_slot_anchor(key, part):
    return slot_layout(key)[0]


def draw_slot_count(key, part):
    return slot_layout(key)[1]


def draw_neighbour(key, part):
    return slot_layout(key)[2]


def draw_root_density(key, part):
    density = jnp.clip(jax.random.normal(jax.random.fold_in(key, 77), (NR, NR, NR), jnp.float32), -6.0, 6.0)
    return density


def steps_of(stream_key, shape, shards, least, high):
    gain = 1.0
    for position, parts in shards:
        steps = jax.random.uniform(jax.random.fold_in(jax.random.fold_in(stream_key, 6), position), (parts,), jnp.float32, least / len(shards), high / len(shards))
        gain = gain * jnp.repeat(jnp.exp(steps), shape[position] // parts).reshape((-1,) + (1,) * (len(shape) - 1 - position))
    return gain


def noise(own_key, extent, spread, most, cuts=(), kind=jnp.bfloat16):
    entries = spread * jax.random.normal(own_key, extent, jnp.float32)
    if cuts:
        entries = entries * steps_of(own_key, extent, cuts, -0.22, 0.18)
    return jnp.clip(entries, -most, most).astype(kind)


def setup_inputs(seed: int = 0) -> dict:
    key_of = jax.random.split(jax.random.key(seed), 7)
    root_density = draw_root_density(jax.random.fold_in(key_of[6], 71), 0)
    subgrid_density = noise(key_of[1], (TOTAL_SLOTS, SUBGRID_CELLS, SUBGRID_CELLS * SUBGRID_CELLS), 4.0, 24.0, ((0, 32),), jnp.float32)
    velocity = noise(key_of[2], (3, TOTAL_SLOTS, SUBGRID_CELLS, SUBGRID_CELLS * SUBGRID_CELLS), 1.0, 6.0, ((1, 32),), jnp.float32)
    slot_anchor = draw_slot_anchor(jax.random.fold_in(key_of[6], 71), 0)
    slot_count = draw_slot_count(jax.random.fold_in(key_of[6], 71), 0)
    neighbour = draw_neighbour(jax.random.fold_in(key_of[6], 71), 0)
    return {"root_density": root_density, "subgrid_density": subgrid_density, "velocity": velocity, "slot_anchor": slot_anchor, "slot_count": slot_count, "neighbour": neighbour}


HIGHEST_PRECISION = lax.Precision.HIGHEST
RELAXATION = 6.0 / 7.0


def eigenvalue(wavenumber):
    return -4.0 * jnp.sin((jnp.pi / NR) * wavenumber.astype(jnp.float32)) ** 2


def green_block(wave_first, wave_second, wave_third):
    total = eigenvalue(wave_first)[:, None, None] + eigenvalue(wave_second)[None, :, None] + eigenvalue(wave_third)[None, None, :]
    zero_mode = (wave_first[:, None, None] == 0) & (wave_second[None, :, None] == 0) & (wave_third[None, None, :] == 0)
    safe_total = jnp.where(zero_mode, -1.0, total)
    return jnp.where(zero_mode, 0.0, 1.0 / safe_total)


def weights_table():
    cells = jnp.arange(REG * REF + 2, dtype=jnp.int32)
    marks = 2 * cells - 1 + REF
    lower_cell = jnp.minimum(marks // (2 * REF), REG)
    fraction = (marks - 2 * REF * lower_cell).astype(jnp.float32) / (2 * REF)
    columns = jnp.arange(REG + 2, dtype=jnp.int32)
    return (jnp.where(columns[None, :] == lower_cell[:, None], 1.0 - fraction[:, None], 0.0)
            + jnp.where(columns[None, :] == lower_cell[:, None] + 1, fraction[:, None], 0.0))


def interpolate(patch, matrix):
    step_one = jnp.einsum("sabc,kc->sabk", patch, matrix, precision=HIGHEST_PRECISION)
    step_two = jnp.einsum("sabk,jb->sajk", step_one, matrix, precision=HIGHEST_PRECISION)
    return jnp.einsum("sajk,ia->sijk", step_two, matrix, precision=HIGHEST_PRECISION)


def extend(coarse, interior, below_face, above_face, use_below, use_above):
    grown = coarse.at[:, 1:-1, 1:-1, 1:-1].set(interior)
    grown = grown.at[:, 1:-1, 0, 1:-1].set(jnp.where(use_below[:, None, None], below_face, grown[:, 1:-1, 0, 1:-1]))
    grown = grown.at[:, 1:-1, -1, 1:-1].set(jnp.where(use_above[:, None, None], above_face, grown[:, 1:-1, -1, 1:-1]))
    return grown


def relax(grown, interior, density):
    beside_all = (grown[:, 2:, 1:-1, 1:-1] + grown[:, :-2, 1:-1, 1:-1]
              + grown[:, 1:-1, 2:, 1:-1] + grown[:, 1:-1, :-2, 1:-1]
              + grown[:, 1:-1, 1:-1, 2:] + grown[:, 1:-1, 1:-1, :-2])
    return (1.0 - RELAXATION) * interior + RELAXATION * (beside_all - density * (1.0 / (REF * REF))) / 6.0


def kick(grown, velocity, live_mask):
    scale_factor = REF / 2.0
    slope_first = (grown[:, 2:, 1:-1, 1:-1] - grown[:, :-2, 1:-1, 1:-1]) * scale_factor
    slope_second = (grown[:, 1:-1, 2:, 1:-1] - grown[:, 1:-1, :-2, 1:-1]) * scale_factor
    slope_third = (grown[:, 1:-1, 1:-1, 2:] - grown[:, 1:-1, 1:-1, :-2]) * scale_factor
    velocity_after_kick = velocity - jnp.stack([slope_first, slope_second, slope_third])
    return jnp.where(live_mask[None, :, None, None, None], velocity_after_kick, 0.0)


def reference(root_density, subgrid_density, velocity, slot_anchor, slot_count, neighbour):
    subgrid_cells = subgrid_density.reshape(TOTAL_SLOTS, SUBGRID_CELLS, SUBGRID_CELLS, SUBGRID_CELLS)
    cell_velocity = velocity.reshape(3, TOTAL_SLOTS, SUBGRID_CELLS, SUBGRID_CELLS, SUBGRID_CELLS)
    every_wave = jnp.arange(NR, dtype=jnp.int32)
    factor = green_block(every_wave, every_wave, every_wave)
    coarse_potential = jnp.real(jnp.fft.ifftn(jnp.fft.fftn(root_density) * factor)).astype(jnp.float32)
    slot_numbers = jnp.arange(TOTAL_SLOTS, dtype=jnp.int32)
    live_mask = (slot_numbers % DEVICE_SLOTS) < slot_count[slot_numbers // DEVICE_SLOTS]
    offsets = jnp.arange(REG + 2, dtype=jnp.int32)
    index_first = (slot_anchor[0][:, None] - 1 + offsets[None, :]) % NR
    index_second = (slot_anchor[1][:, None] - 1 + offsets[None, :]) % NR
    index_third = (slot_anchor[2][:, None] - 1 + offsets[None, :]) % NR
    patch = coarse_potential[index_first[:, :, None, None], index_second[:, None, :, None], index_third[:, None, None, :]]
    coarse = interpolate(patch, weights_table())
    interior = coarse[:, 1:-1, 1:-1, 1:-1]
    below_slot = jnp.maximum(neighbour[0], 0)
    above_slot = jnp.maximum(neighbour[1], 0)
    grown = coarse
    for sweep_index in range(SWEEPS + 1):
        grown = extend(coarse, interior, interior[below_slot, :, -1, :], interior[above_slot, :, 0, :],
                       neighbour[0] >= 0, neighbour[1] >= 0)
        if sweep_index < SWEEPS:
            interior = relax(grown, interior, subgrid_cells)
    subgrid_potential = jnp.where(live_mask[:, None, None, None], interior, 0.0)
    velocity_after_kick = kick(grown, cell_velocity, live_mask)
    return (coarse_potential, subgrid_potential.reshape(TOTAL_SLOTS, SUBGRID_CELLS, SUBGRID_CELLS * SUBGRID_CELLS),
            velocity_after_kick.reshape(3, TOTAL_SLOTS, SUBGRID_CELLS, SUBGRID_CELLS * SUBGRID_CELLS))
```

```python
import jax
import jax.numpy as jnp
import numpy as np
from jax import lax
from jax.experimental import pallas as pl
from jax.experimental.pallas import tpu as pltpu
from jax.sharding import PartitionSpec as P

NR = 384
REG = 8
REF = 4
SWEEPS = 4
CELLS = REG * REF
EDGE = SWEEPS
LAYERS = CELLS + 2 * EDGE
WIDE = LAYERS * CELLS
RELAXATION = 6.0 / 7.0
HIGHEST = lax.Precision.HIGHEST
HIGH = lax.Precision.HIGH
F32 = jnp.float32


def fourier_basis(length):
    cell = np.arange(length)
    rows = []
    for k in range(length):
        if k in (0, length // 2):
            rows.append(np.cos(2 * np.pi * (k * cell % length) / length) / np.sqrt(length))
        elif k < length // 2:
            rows.append(np.cos(2 * np.pi * (k * cell % length) / length) * np.sqrt(2 / length))
        else:
            rows.append(
                np.sin(2 * np.pi * ((length - k) * cell % length) / length) * np.sqrt(2 / length)
            )
    return np.stack(rows)


def pseudo_inverse(length):
    basis = fourier_basis(length)
    eig = -4 * np.sin(np.pi * np.arange(length) / length) ** 2
    scale = np.where(np.arange(length) == 0, 0.0, 1 / np.where(eig == 0, -1.0, eig))
    return (basis.T * scale) @ basis


def axis_weights(cells, first, count):
    table = np.zeros((len(cells), count))
    for row, cell in enumerate(cells):
        mark = 2 * cell - 1 + REF
        low = mark // (2 * REF)
        frac = (mark - 2 * REF * low) / (2 * REF)
        table[row, low - first] += 1 - frac
        if frac:
            table[row, low + 1 - first] += frac
    return table


PATCH_X = REG + 2
PATCH_Y = REG + 4
PATCH_Z = REG + 2


def patch_tables():
    inner = np.arange(1, CELLS + 1)
    x_side = axis_weights(np.concatenate([inner, [0, CELLS + 1]]), 0, PATCH_X)
    x_table = np.zeros((CELLS + 8, 16))
    x_table[: CELLS + 2, :PATCH_X] = x_side
    y_cells = np.arange(1 - EDGE, CELLS + EDGE + 1)
    y_side = axis_weights(y_cells, -1, PATCH_Y)
    y_out = axis_weights(np.array([-EDGE, CELLS + EDGE + 1]), -1, PATCH_Y)
    z_side = axis_weights(np.arange(CELLS + 2), 0, PATCH_Z)
    z_edge = np.zeros((CELLS, PATCH_Z))
    z_edge[0] = z_side[0]
    z_edge[-1] = z_side[-1]
    y_edge = np.zeros((LAYERS, PATCH_Y))
    y_edge[0] = y_out[0]
    y_edge[-1] = y_out[1]

    def both(ys, zs):
        return np.einsum("jb,kc->bcjk", ys, zs).reshape(PATCH_Y * PATCH_Z, WIDE)

    table = np.zeros((128, 3 * WIDE))
    table[: PATCH_Y * PATCH_Z] = np.concatenate(
        [both(y_side, z_side[1:-1]), both(y_side, z_edge), both(y_edge, z_side[1:-1])], axis=1
    )
    return x_table.astype(np.float32), table.astype(np.float32)


def from_behind(value, axis, steps):
    count = lax.axis_size(axis)
    initial, last = (max(0, -steps), min(count, count - steps))
    return lax.ppermute(value, axis, [(source, source + steps) for source in range(initial, last)])


def extended(block, axis, dim, width):
    count = lax.axis_size(axis)
    forward = [(i, (i + 1) % count) for i in range(count)]
    backward = [(target, source) for source, target in forward]
    low = lax.ppermute(
        lax.slice_in_dim(block, block.shape[dim] - width, None, axis=dim), axis, forward
    )
    high = lax.ppermute(lax.slice_in_dim(block, 0, width, axis=dim), axis, backward)
    return jnp.concatenate([low, block, high], axis=dim)


def decay(length, eig_first, eig_second):
    delta = -(eig_first + eig_second)
    delta = jnp.where(delta <= 0.0, 1.0, delta)
    q = 0.5 * delta + jnp.sqrt(delta + 0.25 * delta * delta)
    return 1.0 / (1.0 + q)


def moments_kernel(f_ref, eb_ref, ec_ref, out_ref):
    rows = f_ref.shape[0]
    r = decay(NR, eb_ref[...], ec_ref[...])
    up = f_ref[0]
    down = f_ref[rows - 1]
    for i in range(1, rows):
        up = r * up + f_ref[i]
        down = r * down + f_ref[rows - 1 - i]
    out_ref[0] = up
    out_ref[1] = down


def carry_kernel(rows, mom_ref, eb_ref, ec_ref, out_ref):
    blocks = mom_ref.shape[0]
    band = out_ref.shape[1] // 2
    r = decay(NR, eb_ref[...], ec_ref[...])
    ratio = r
    for _ in range(rows - 1):
        ratio = ratio * r
    total = jnp.ones_like(ratio)
    up = jnp.zeros_like(ratio)
    down = jnp.zeros_like(ratio)
    for k in range(blocks):
        total = total * ratio
        up = ratio * up + mom_ref[k, :band]
        down = ratio * down + mom_ref[blocks - 1 - k, band : 2 * band]
    norm = 1.0 / (1.0 - total)
    up = up * norm
    down = down * norm
    for k in range(blocks):
        out_ref[k, :band] = up
        up = ratio * up + mom_ref[k, :band]
        other = blocks - 1 - k
        out_ref[other, band : 2 * band] = down
        down = ratio * down + mom_ref[other, band : 2 * band]


def solve_kernel(f_ref, carry_ref, eb_ref, ec_ref, zero_ref, out_ref):
    rows = f_ref.shape[0]
    r = decay(NR, eb_ref[...], ec_ref[...])
    scale = -r / ((1.0 - r) * (1.0 + r))
    tile = f_ref.shape[1]
    first = lax.broadcasted_iota(jnp.int32, r.shape, 0) + pl.program_id(0) * tile
    second = lax.broadcasted_iota(jnp.int32, r.shape, 1)
    zero_mode = (first == 0) & (second == 0)
    up = carry_ref[0]
    for i in range(rows):
        up = r * up + f_ref[i]
        out_ref[i] = up
    down = carry_ref[1]
    for i in range(rows - 1, -1, -1):
        down = r * down
        value = (out_ref[i] + down) * scale
        out_ref[i] = jnp.where(zero_mode, zero_ref[i][None, :], value)
        down = down + f_ref[i]


def subgrid_kernel(
    flag_ref, patch_ref, xt_ref, yz_ref, mid_ref, low_ref, high_ref, vel_ref, pot_ref, kick_ref
):
    slot = pl.program_id(0)
    live = flag_ref[0, slot] > 0
    has_below = flag_ref[1, slot] > 0
    has_above = flag_ref[2, slot] > 0
    back_below = flag_ref[3, slot] > 0
    back_above = flag_ref[4, slot] > 0
    planes = jnp.dot(patch_ref[0], yz_ref[...], precision=HIGHEST, preferred_element_type=F32)
    coarse = jnp.dot(xt_ref[...], planes, precision=HIGHEST, preferred_element_type=F32)
    start = coarse[:CELLS, :WIDE]
    x_low = coarse[CELLS : CELLS + 1, :WIDE]
    x_high = coarse[CELLS + 1 : CELLS + 2, :WIDE]
    z_edge = coarse[:CELLS, WIDE : 2 * WIDE]
    y_edge = coarse[:CELLS, 2 * WIDE :]
    shape = (CELLS, WIDE)
    row = lax.broadcasted_iota(jnp.int32, shape, 0)
    lane = lax.broadcasted_iota(jnp.int32, shape, 1)
    third = lane % CELLS
    side = EDGE * CELLS
    end = WIDE - side
    y_above = jnp.where(lane >= WIDE - CELLS, y_edge, pltpu.roll(start, WIDE - CELLS, 1))
    y_below = jnp.where(lane < CELLS, y_edge, pltpu.roll(start, CELLS, 1))
    cut_above = (lane >= WIDE - CELLS) | (
        (lane >= side - CELLS) & (lane < side) & jnp.logical_not(back_below)
    )
    cut_below = (lane < CELLS) | (
        (lane >= end) & (lane < end + CELLS) & jnp.logical_not(back_above)
    )
    fixed = ((lane < side) & jnp.logical_not(has_below)) | (
        (lane >= end) & jnp.logical_not(has_above)
    )
    rho = jnp.concatenate([low_ref[0], mid_ref[0], high_ref[0]], axis=1) * (1.0 / (REF * REF))

    def beside(v):
        return (
            (
                jnp.where(row == 0, x_low, pltpu.roll(v, 1, 0)),
                jnp.where(row == CELLS - 1, x_high, pltpu.roll(v, CELLS - 1, 0)),
            ),
            (
                jnp.where(cut_below, y_below, pltpu.roll(v, CELLS, 1)),
                jnp.where(cut_above, y_above, pltpu.roll(v, WIDE - CELLS, 1)),
            ),
            (
                jnp.where(third == 0, z_edge, pltpu.roll(v, 1, 1)),
                jnp.where(third == CELLS - 1, z_edge, pltpu.roll(v, WIDE - 1, 1)),
            ),
        )

    v = start
    for _ in range(SWEEPS):
        first, second, last = beside(v)
        total = first[1] + first[0] + second[1] + second[0] + last[1] + last[0]
        new = (1.0 - RELAXATION) * v + RELAXATION * (total - rho) / 6.0
        v = jnp.where(fixed, v, new)
    pot_ref[0] = jnp.where(live, v[:, side:end], 0.0)
    for q, (below, above) in enumerate(beside(v)):
        slope = (above[:, side:end] - below[:, side:end]) * (REF / 2.0)
        kick_ref[q, 0] = jnp.where(live, vel_ref[q, 0] - slope, 0.0)


def poisson(root_density):
    size_second = lax.axis_size("py")
    devices = lax.axis_size("px") * size_second
    device = lax.axis_index("px") * size_second + lax.axis_index("py")
    basis = jnp.asarray(fourier_basis(NR), F32)
    eig = -4.0 * np.sin(np.pi / NR * np.arange(NR)) ** 2
    eig_first = jnp.asarray(eig[:, None], F32)
    eig_second = jnp.asarray(eig[None, :], F32)
    rows = NR // devices
    band = NR // devices
    planes = lax.all_to_all(root_density, "py", split_axis=0, concat_axis=1, tiled=True)
    f = jnp.einsum("xyz,cz->xyc", planes, basis, precision=HIGH)
    f = jnp.einsum("xyc,by->xbc", f, basis, precision=HIGH)
    tile = 48
    grid = NR // tile
    f_spec = pl.BlockSpec((rows, tile, NR), lambda t: (0, t, 0))
    pair_spec = pl.BlockSpec((2, tile, NR), lambda t: (0, t, 0))
    eb_spec = pl.BlockSpec((tile, 1), lambda t: (t, 0))
    ec_spec = pl.BlockSpec((1, NR), lambda t: (0, 0))
    params = pltpu.CompilerParams(
        dimension_semantics=("arbitrary",), vmem_limit_bytes=60 * 1024 * 1024
    )
    moments = pl.pallas_call(
        moments_kernel,
        grid=(grid,),
        in_specs=[f_spec, eb_spec, ec_spec],
        out_specs=pair_spec,
        out_shape=jax.ShapeDtypeStruct((2, NR, NR), F32),
        compiler_params=params,
    )(f, eig_first, eig_second)
    column = jnp.pad(f[:, 0, 0], (0, NR - rows))
    sent = jnp.concatenate(
        [
            moments.reshape(2, devices, band, NR).transpose(1, 0, 2, 3).reshape(
                devices, 2 * band, NR
            ),
            jnp.broadcast_to(column[None, None, :], (devices, 8, NR)),
        ],
        axis=1,
    )
    got = lax.all_to_all(sent, ("px", "py"), split_axis=0, concat_axis=0, tiled=True)
    carries = pl.pallas_call(
        lambda *refs: carry_kernel(rows, *refs),
        out_shape=jax.ShapeDtypeStruct((devices, 2 * band, NR), F32),
        compiler_params=pltpu.CompilerParams(vmem_limit_bytes=60 * 1024 * 1024),
    )(got, lax.dynamic_slice_in_dim(eig_first, device * band, band, 0), eig_second)
    back = lax.all_to_all(carries, ("px", "py"), split_axis=0, concat_axis=0, tiled=True)
    back = back.reshape(devices, 2, band, NR).transpose(1, 0, 2, 3).reshape(2, NR, NR)
    whole_column = got[:, 2 * band, :rows].reshape(NR)
    own = lax.dynamic_slice_in_dim(
        jnp.asarray(pseudo_inverse(NR), F32), device * rows, rows, 0
    )
    zero_values = jnp.sum(own * whole_column[None, :], axis=1)
    zero_wide = jnp.broadcast_to(zero_values[:, None], (rows, NR))
    u = pl.pallas_call(
        solve_kernel,
        grid=(grid,),
        in_specs=[f_spec, pair_spec, eb_spec, ec_spec, pl.BlockSpec((rows, NR), lambda t: (0, 0))],
        out_specs=f_spec,
        out_shape=jax.ShapeDtypeStruct((rows, NR, NR), F32),
        compiler_params=params,
    )(f, back, eig_first, eig_second, zero_wide)
    u = jnp.einsum("xbc,by->xyc", u, basis, precision=HIGH)
    u = jnp.einsum("xyc,cz->xyz", u, basis, precision=HIGH)
    return lax.all_to_all(u, "py", split_axis=1, concat_axis=0, tiled=True)


def local(root_density, subgrid_density, velocity, slot_anchor, slot_count, neighbour):
    first_rows, second_rows = root_density.shape[:2]
    size_second = lax.axis_size("py")
    place_first = lax.axis_index("px")
    place_second = lax.axis_index("py")
    device = place_first * size_second + place_second
    per_device = subgrid_density.shape[0]
    side = EDGE * CELLS
    inner = CELLS * CELLS
    low_density = from_behind(subgrid_density[:, :, inner - side :], "py", 1)
    high_density = from_behind(subgrid_density[:, :, :side], "py", -1)
    coarse_potential = poisson(root_density)
    padded = extended(extended(coarse_potential, "px", 0, 1), "py", 1, 2)
    patches = []
    for target in range(size_second):
        owner = place_first * size_second + target
        wanted = (place_second - target) % size_second
        anchor = slot_anchor[:, owner * per_device + wanted]
        x = jnp.clip(anchor[0] - place_first * first_rows, 0, first_rows - REG)
        y = jnp.clip(anchor[1] - place_second * second_rows, 0, second_rows - REG)
        cut = lax.dynamic_slice(padded, (x, y, 0), (PATCH_X, PATCH_Y, NR))
        columns = (anchor[2] - 1 + jnp.arange(PATCH_Z, dtype=jnp.int32)) % NR
        pick = (jnp.arange(NR, dtype=jnp.int32)[:, None] == columns[None, :]).astype(F32)
        patches.append(
            jnp.dot(cut.reshape(PATCH_X * PATCH_Y, NR), pick, precision=HIGHEST).reshape(-1)
        )
    arrived = lax.all_to_all(
        jnp.stack(patches), "py", split_axis=0, concat_axis=0, tiled=True
    )
    positions = jnp.arange(per_device, dtype=jnp.int32)
    patch = arrived[(place_second + positions) % size_second]
    patch = patch.reshape(per_device, PATCH_X, PATCH_Y * PATCH_Z)
    patch = jnp.pad(
        patch, ((0, 0), (0, 16 - PATCH_X), (0, 128 - PATCH_Y * PATCH_Z))
    )
    slots = device * per_device + positions
    below, above = neighbour[0][slots], neighbour[1][slots]
    flags = jnp.stack(
        [
            positions < slot_count[device],
            below >= 0,
            above >= 0,
            neighbour[1][jnp.maximum(below, 0)] >= 0,
            neighbour[0][jnp.maximum(above, 0)] >= 0,
        ]
    ).astype(jnp.int32)
    x_table, yz_table = patch_tables()
    slot_spec = lambda width: pl.BlockSpec((1, CELLS, width), lambda s: (s, 0, 0))
    vel_spec = pl.BlockSpec((3, 1, CELLS, inner), lambda s: (0, s, 0, 0))
    potential, kicked = pl.pallas_call(
        subgrid_kernel,
        grid=(per_device,),
        in_specs=[
            pl.BlockSpec(memory_space=pltpu.SMEM),
            pl.BlockSpec((1, 16, 128), lambda s: (s, 0, 0)),
            pl.BlockSpec(x_table.shape, lambda s: (0, 0)),
            pl.BlockSpec(yz_table.shape, lambda s: (0, 0)),
            slot_spec(inner),
            slot_spec(side),
            slot_spec(side),
            vel_spec,
        ],
        out_specs=[slot_spec(inner), vel_spec],
        out_shape=[
            jax.ShapeDtypeStruct(subgrid_density.shape, F32),
            jax.ShapeDtypeStruct(velocity.shape, F32),
        ],
        compiler_params=pltpu.CompilerParams(
            dimension_semantics=("arbitrary",), vmem_limit_bytes=60 * 1024 * 1024
        ),
    )(
        flags,
        patch,
        jnp.asarray(x_table),
        jnp.asarray(yz_table),
        subgrid_density,
        low_density,
        high_density,
        velocity,
    )
    return (coarse_potential, potential, kicked)


def solution(mesh):
    return jax.shard_map(
        local,
        mesh=mesh,
        in_specs=(
            P("px", "py", None),
            P(("px", "py"), None, None),
            P(None, ("px", "py"), None, None),
            P(),
            P(),
            P(),
        ),
        out_specs=(
            P("px", "py", None),
            P(("px", "py"), None, None),
            P(None, ("px", "py"), None, None),
        ),
        check_vma=False,
    )
```

```python
import jax
import jax.numpy as jnp
import numpy as np
from jax import lax
from jax.experimental import pallas as pl
from jax.experimental.pallas import tpu as pltpu
from jax.sharding import PartitionSpec as P

NR = 384
REG = 8
REF = 4
SWEEPS = 4
CELLS = REG * REF
EDGE = SWEEPS
LAYERS = CELLS + 2 * EDGE
WIDE = LAYERS * CELLS
RELAXATION = 6.0 / 7.0
HIGHEST = lax.Precision.HIGHEST
HIGH = lax.Precision.HIGH
F32 = jnp.float32


def fourier_basis(length):
    cell = np.arange(length)
    rows = []
    for k in range(length):
        if k in (0, length // 2):
            rows.append(np.cos(2 * np.pi * (k * cell % length) / length) / np.sqrt(length))
        elif k < length // 2:
            rows.append(np.cos(2 * np.pi * (k * cell % length) / length) * np.sqrt(2 / length))
        else:
            rows.append(
                np.sin(2 * np.pi * ((length - k) * cell % length) / length) * np.sqrt(2 / length)
            )
    return np.stack(rows)


def pseudo_inverse(length):
    basis = fourier_basis(length)
    eig = -4 * np.sin(np.pi * np.arange(length) / length) ** 2
    scale = np.where(np.arange(length) == 0, 0.0, 1 / np.where(eig == 0, -1.0, eig))
    return (basis.T * scale) @ basis


def axis_weights(cells, first, count):
    table = np.zeros((len(cells), count))
    for row, cell in enumerate(cells):
        mark = 2 * cell - 1 + REF
        low = mark // (2 * REF)
        frac = (mark - 2 * REF * low) / (2 * REF)
        table[row, low - first] += 1 - frac
        if frac:
            table[row, low + 1 - first] += frac
    return table


PATCH_X = REG + 2
PATCH_Y = REG + 4
PATCH_Z = REG + 2


def patch_tables():
    inner = np.arange(1, CELLS + 1)
    x_side = axis_weights(np.concatenate([inner, [0, CELLS + 1]]), 0, PATCH_X)
    x_table = np.zeros((CELLS + 8, 16))
    x_table[: CELLS + 2, :PATCH_X] = x_side
    y_cells = np.arange(1 - EDGE, CELLS + EDGE + 1)
    y_side = axis_weights(y_cells, -1, PATCH_Y)
    y_out = axis_weights(np.array([-EDGE, CELLS + EDGE + 1]), -1, PATCH_Y)
    z_side = axis_weights(np.arange(CELLS + 2), 0, PATCH_Z)
    z_edge = np.zeros((CELLS, PATCH_Z))
    z_edge[0] = z_side[0]
    z_edge[-1] = z_side[-1]
    y_edge = np.zeros((LAYERS, PATCH_Y))
    y_edge[0] = y_out[0]
    y_edge[-1] = y_out[1]

    def both(ys, zs):
        return np.einsum("jb,kc->bcjk", ys, zs).reshape(PATCH_Y * PATCH_Z, WIDE)

    table = np.zeros((128, 3 * WIDE))
    table[: PATCH_Y * PATCH_Z] = np.concatenate(
        [both(y_side, z_side[1:-1]), both(y_side, z_edge), both(y_edge, z_side[1:-1])], axis=1
    )
    return x_table.astype(np.float32), table.astype(np.float32)


def from_behind(value, axis, steps):
    count = lax.axis_size(axis)
    initial, last = (max(0, -steps), min(count, count - steps))
    return lax.ppermute(value, axis, [(source, source + steps) for source in range(initial, last)])


def extended(block, axis, dim, width):
    count = lax.axis_size(axis)
    forward = [(i, (i + 1) % count) for i in range(count)]
    backward = [(target, source) for source, target in forward]
    low = lax.ppermute(
        lax.slice_in_dim(block, block.shape[dim] - width, None, axis=dim), axis, forward
    )
    high = lax.ppermute(lax.slice_in_dim(block, 0, width, axis=dim), axis, backward)
    return jnp.concatenate([low, block, high], axis=dim)


def decay(length, eig_first, eig_second):
    delta = -(eig_first + eig_second)
    delta = jnp.where(delta <= 0.0, 1.0, delta)
    q = 0.5 * delta + jnp.sqrt(delta + 0.25 * delta * delta)
    return 1.0 / (1.0 + q)


def moments_kernel(f_ref, eb_ref, ec_ref, out_ref):
    rows = f_ref.shape[0]
    r = decay(NR, eb_ref[...], ec_ref[...])
    up = f_ref[0]
    down = f_ref[rows - 1]
    for i in range(1, rows):
        up = r * up + f_ref[i]
        down = r * down + f_ref[rows - 1 - i]
    out_ref[0] = up
    out_ref[1] = down


def carry_kernel(rows, order, mom_ref, eb_ref, ec_ref, out_ref):
    blocks = mom_ref.shape[0]
    band = out_ref.shape[1] // 2
    r = decay(NR, eb_ref[...], ec_ref[...])
    ratio = r
    for _ in range(rows - 1):
        ratio = ratio * r
    total = jnp.ones_like(ratio)
    up = jnp.zeros_like(ratio)
    down = jnp.zeros_like(ratio)
    for k in range(blocks):
        total = total * ratio
        up = ratio * up + mom_ref[order[k], :band]
        down = ratio * down + mom_ref[order[blocks - 1 - k], band : 2 * band]
    norm = 1.0 / (1.0 - total)
    up = up * norm
    down = down * norm
    for k in range(blocks):
        out_ref[order[k], :band] = up
        up = ratio * up + mom_ref[order[k], :band]
        other = order[blocks - 1 - k]
        out_ref[other, band : 2 * band] = down
        down = ratio * down + mom_ref[other, band : 2 * band]


def solve_kernel(f_ref, carry_ref, eb_ref, ec_ref, zero_ref, out_ref):
    rows = f_ref.shape[0]
    r = decay(NR, eb_ref[...], ec_ref[...])
    scale = -r / ((1.0 - r) * (1.0 + r))
    tile = f_ref.shape[1]
    first = lax.broadcasted_iota(jnp.int32, r.shape, 0) + pl.program_id(0) * tile
    second = lax.broadcasted_iota(jnp.int32, r.shape, 1)
    zero_mode = (first == 0) & (second == 0)
    up = carry_ref[0]
    for i in range(rows):
        up = r * up + f_ref[i]
        out_ref[i] = up
    down = carry_ref[1]
    for i in range(rows - 1, -1, -1):
        down = r * down
        value = (out_ref[i] + down) * scale
        out_ref[i] = jnp.where(zero_mode, zero_ref[i][None, :], value)
        down = down + f_ref[i]


def subgrid_kernel(
    flag_ref, patch_ref, xt_ref, yz_ref, mid_ref, low_ref, high_ref, vel_ref, pot_ref, kick_ref
):
    slot = pl.program_id(0)
    live = flag_ref[0, slot] > 0
    has_below = flag_ref[1, slot] > 0
    has_above = flag_ref[2, slot] > 0
    back_below = flag_ref[3, slot] > 0
    back_above = flag_ref[4, slot] > 0
    planes = jnp.dot(patch_ref[0], yz_ref[...], precision=HIGHEST, preferred_element_type=F32)
    coarse = jnp.dot(xt_ref[...], planes, precision=HIGHEST, preferred_element_type=F32)
    start = coarse[:CELLS, :WIDE]
    x_low = coarse[CELLS : CELLS + 1, :WIDE]
    x_high = coarse[CELLS + 1 : CELLS + 2, :WIDE]
    z_edge = coarse[:CELLS, WIDE : 2 * WIDE]
    y_edge = coarse[:CELLS, 2 * WIDE :]
    shape = (CELLS, WIDE)
    row = lax.broadcasted_iota(jnp.int32, shape, 0)
    lane = lax.broadcasted_iota(jnp.int32, shape, 1)
    third = lane % CELLS
    side = EDGE * CELLS
    end = WIDE - side
    y_above = jnp.where(lane >= WIDE - CELLS, y_edge, pltpu.roll(start, WIDE - CELLS, 1))
    y_below = jnp.where(lane < CELLS, y_edge, pltpu.roll(start, CELLS, 1))
    cut_above = (lane >= WIDE - CELLS) | (
        (lane >= side - CELLS) & (lane < side) & jnp.logical_not(back_below)
    )
    cut_below = (lane < CELLS) | (
        (lane >= end) & (lane < end + CELLS) & jnp.logical_not(back_above)
    )
    fixed = ((lane < side) & jnp.logical_not(has_below)) | (
        (lane >= end) & jnp.logical_not(has_above)
    )
    rho = jnp.concatenate([low_ref[0], mid_ref[0], high_ref[0]], axis=1) * (1.0 / (REF * REF))

    def beside(v):
        return (
            (
                jnp.where(row == 0, x_low, pltpu.roll(v, 1, 0)),
                jnp.where(row == CELLS - 1, x_high, pltpu.roll(v, CELLS - 1, 0)),
            ),
            (
                jnp.where(cut_below, y_below, pltpu.roll(v, CELLS, 1)),
                jnp.where(cut_above, y_above, pltpu.roll(v, WIDE - CELLS, 1)),
            ),
            (
                jnp.where(third == 0, z_edge, pltpu.roll(v, 1, 1)),
                jnp.where(third == CELLS - 1, z_edge, pltpu.roll(v, WIDE - 1, 1)),
            ),
        )

    v = start
    for _ in range(SWEEPS):
        first, second, last = beside(v)
        total = first[1] + first[0] + second[1] + second[0] + last[1] + last[0]
        new = (1.0 - RELAXATION) * v + RELAXATION * (total - rho) / 6.0
        v = jnp.where(fixed, v, new)
    pot_ref[0] = jnp.where(live, v[:, side:end], 0.0)
    for q, (below, above) in enumerate(beside(v)):
        slope = (above[:, side:end] - below[:, side:end]) * (REF / 2.0)
        kick_ref[q, 0] = jnp.where(live, vel_ref[q, 0] - slope, 0.0)


def poisson(root_density):
    size_first = lax.axis_size("px")
    size_second = lax.axis_size("py")
    devices = size_first * size_second
    device = lax.axis_index("px") * size_second + lax.axis_index("py")
    block = lax.axis_index("py") * size_first + lax.axis_index("px")
    order = [(k % size_first) * size_second + k // size_first for k in range(devices)]
    basis = jnp.asarray(fourier_basis(NR), F32)
    eig = -4.0 * np.sin(np.pi / NR * np.arange(NR)) ** 2
    eig_first = jnp.asarray(eig[:, None], F32)
    eig_second = jnp.asarray(eig[None, :], F32)
    rows = NR // devices
    band = NR // devices
    planes = lax.all_to_all(
        jnp.transpose(root_density, (1, 0, 2)), "px", split_axis=0, concat_axis=1, tiled=True
    )
    f = jnp.einsum("yxz,cz->yxc", planes, basis, precision=HIGH)
    f = jnp.einsum("yxc,ax->yac", f, basis, precision=HIGH)
    tile = 48
    grid = NR // tile
    f_spec = pl.BlockSpec((rows, tile, NR), lambda t: (0, t, 0))
    pair_spec = pl.BlockSpec((2, tile, NR), lambda t: (0, t, 0))
    eb_spec = pl.BlockSpec((tile, 1), lambda t: (t, 0))
    ec_spec = pl.BlockSpec((1, NR), lambda t: (0, 0))
    params = pltpu.CompilerParams(
        dimension_semantics=("arbitrary",), vmem_limit_bytes=60 * 1024 * 1024
    )
    moments = pl.pallas_call(
        moments_kernel,
        grid=(grid,),
        in_specs=[f_spec, eb_spec, ec_spec],
        out_specs=pair_spec,
        out_shape=jax.ShapeDtypeStruct((2, NR, NR), F32),
        compiler_params=params,
    )(f, eig_first, eig_second)
    column = jnp.pad(f[:, 0, 0], (0, NR - rows))
    sent = jnp.concatenate(
        [
            moments.reshape(2, devices, band, NR).transpose(1, 0, 2, 3).reshape(
                devices, 2 * band, NR
            ),
            jnp.broadcast_to(column[None, None, :], (devices, 8, NR)),
        ],
        axis=1,
    )
    got = lax.all_to_all(sent, ("px", "py"), split_axis=0, concat_axis=0, tiled=True)
    carries = pl.pallas_call(
        lambda *refs: carry_kernel(rows, order, *refs),
        out_shape=jax.ShapeDtypeStruct((devices, 2 * band, NR), F32),
        compiler_params=pltpu.CompilerParams(vmem_limit_bytes=60 * 1024 * 1024),
    )(got, lax.dynamic_slice_in_dim(eig_first, device * band, band, 0), eig_second)
    back = lax.all_to_all(carries, ("px", "py"), split_axis=0, concat_axis=0, tiled=True)
    back = back.reshape(devices, 2, band, NR).transpose(1, 0, 2, 3).reshape(2, NR, NR)
    whole_column = got[:, 2 * band, :rows].reshape(size_first, size_second, rows)
    whole_column = whole_column.transpose(1, 0, 2).reshape(NR)
    own = lax.dynamic_slice_in_dim(
        jnp.asarray(pseudo_inverse(NR), F32), block * rows, rows, 0
    )
    zero_values = jnp.sum(own * whole_column[None, :], axis=1)
    zero_wide = jnp.broadcast_to(zero_values[:, None], (rows, NR))
    u = pl.pallas_call(
        solve_kernel,
        grid=(grid,),
        in_specs=[f_spec, pair_spec, eb_spec, ec_spec, pl.BlockSpec((rows, NR), lambda t: (0, 0))],
        out_specs=f_spec,
        out_shape=jax.ShapeDtypeStruct((rows, NR, NR), F32),
        compiler_params=params,
    )(f, back, eig_first, eig_second, zero_wide)
    u = jnp.einsum("yac,ax->yxc", u, basis, precision=HIGH)
    u = jnp.einsum("yxc,cz->yxz", u, basis, precision=HIGH)
    u = lax.all_to_all(u, "px", split_axis=1, concat_axis=0, tiled=True)
    return jnp.transpose(u, (1, 0, 2))


def local(root_density, subgrid_density, velocity, slot_anchor, slot_count, neighbour):
    first_rows, second_rows = root_density.shape[:2]
    size_second = lax.axis_size("py")
    place_first = lax.axis_index("px")
    place_second = lax.axis_index("py")
    device = place_first * size_second + place_second
    per_device = subgrid_density.shape[0]
    side = EDGE * CELLS
    inner = CELLS * CELLS
    low_density = from_behind(subgrid_density[:, :, inner - side :], "py", 1)
    high_density = from_behind(subgrid_density[:, :, :side], "py", -1)
    coarse_potential = poisson(root_density)
    padded = extended(extended(coarse_potential, "px", 0, 1), "py", 1, 2)
    patches = []
    for target in range(size_second):
        owner = place_first * size_second + target
        wanted = (place_second - target) % size_second
        anchor = slot_anchor[:, owner * per_device + wanted]
        x = jnp.clip(anchor[0] - place_first * first_rows, 0, first_rows - REG)
        y = jnp.clip(anchor[1] - place_second * second_rows, 0, second_rows - REG)
        cut = lax.dynamic_slice(padded, (x, y, 0), (PATCH_X, PATCH_Y, NR))
        columns = (anchor[2] - 1 + jnp.arange(PATCH_Z, dtype=jnp.int32)) % NR
        pick = (jnp.arange(NR, dtype=jnp.int32)[:, None] == columns[None, :]).astype(F32)
        patches.append(
            jnp.dot(cut.reshape(PATCH_X * PATCH_Y, NR), pick, precision=HIGHEST).reshape(-1)
        )
    arrived = lax.all_to_all(
        jnp.stack(patches), "py", split_axis=0, concat_axis=0, tiled=True
    )
    positions = jnp.arange(per_device, dtype=jnp.int32)
    patch = arrived[(place_second + positions) % size_second]
    patch = patch.reshape(per_device, PATCH_X, PATCH_Y * PATCH_Z)
    patch = jnp.pad(
        patch, ((0, 0), (0, 16 - PATCH_X), (0, 128 - PATCH_Y * PATCH_Z))
    )
    slots = device * per_device + positions
    below, above = neighbour[0][slots], neighbour[1][slots]
    flags = jnp.stack(
        [
            positions < slot_count[device],
            below >= 0,
            above >= 0,
            neighbour[1][jnp.maximum(below, 0)] >= 0,
            neighbour[0][jnp.maximum(above, 0)] >= 0,
        ]
    ).astype(jnp.int32)
    x_table, yz_table = patch_tables()
    slot_spec = lambda width: pl.BlockSpec((1, CELLS, width), lambda s: (s, 0, 0))
    vel_spec = pl.BlockSpec((3, 1, CELLS, inner), lambda s: (0, s, 0, 0))
    potential, kicked = pl.pallas_call(
        subgrid_kernel,
        grid=(per_device,),
        in_specs=[
            pl.BlockSpec(memory_space=pltpu.SMEM),
            pl.BlockSpec((1, 16, 128), lambda s: (s, 0, 0)),
            pl.BlockSpec(x_table.shape, lambda s: (0, 0)),
            pl.BlockSpec(yz_table.shape, lambda s: (0, 0)),
            slot_spec(inner),
            slot_spec(side),
            slot_spec(side),
            vel_spec,
        ],
        out_specs=[slot_spec(inner), vel_spec],
        out_shape=[
            jax.ShapeDtypeStruct(subgrid_density.shape, F32),
            jax.ShapeDtypeStruct(velocity.shape, F32),
        ],
        compiler_params=pltpu.CompilerParams(
            dimension_semantics=("arbitrary",), vmem_limit_bytes=60 * 1024 * 1024
        ),
    )(
        flags,
        patch,
        jnp.asarray(x_table),
        jnp.asarray(yz_table),
        subgrid_density,
        low_density,
        high_density,
        velocity,
    )
    return (coarse_potential, potential, kicked)


def solution(mesh):
    return jax.shard_map(
        local,
        mesh=mesh,
        in_specs=(
            P("px", "py", None),
            P(("px", "py"), None, None),
            P(None, ("px", "py"), None, None),
            P(),
            P(),
            P(),
        ),
        out_specs=(
            P("px", "py", None),
            P(("px", "py"), None, None),
            P(None, ("px", "py"), None, None),
        ),
        check_vma=False,
    )
```

```python
import jax
import jax.numpy as jnp
import numpy as np
from jax import lax
from jax.experimental import pallas as pl
from jax.experimental.pallas import tpu as pltpu
from jax.sharding import PartitionSpec as P

NR = 384
REG = 8
REF = 4
SWEEPS = 4
CELLS = REG * REF
EDGE = SWEEPS
LAYERS = CELLS + 2 * EDGE
WIDE = LAYERS * CELLS
RELAXATION = 6.0 / 7.0
HIGHEST = lax.Precision.HIGHEST
HIGH = lax.Precision.HIGH
F32 = jnp.float32


def fourier_basis(length):
    cell = np.arange(length)
    rows = []
    for k in range(length):
        if k in (0, length // 2):
            rows.append(np.cos(2 * np.pi * (k * cell % length) / length) / np.sqrt(length))
        elif k < length // 2:
            rows.append(np.cos(2 * np.pi * (k * cell % length) / length) * np.sqrt(2 / length))
        else:
            rows.append(
                np.sin(2 * np.pi * ((length - k) * cell % length) / length) * np.sqrt(2 / length)
            )
    return np.stack(rows)


def pseudo_inverse(length):
    basis = fourier_basis(length)
    eig = -4 * np.sin(np.pi * np.arange(length) / length) ** 2
    scale = np.where(np.arange(length) == 0, 0.0, 1 / np.where(eig == 0, -1.0, eig))
    return (basis.T * scale) @ basis


def axis_weights(cells, first, count):
    table = np.zeros((len(cells), count))
    for row, cell in enumerate(cells):
        mark = 2 * cell - 1 + REF
        low = mark // (2 * REF)
        frac = (mark - 2 * REF * low) / (2 * REF)
        table[row, low - first] += 1 - frac
        if frac:
            table[row, low + 1 - first] += frac
    return table


PATCH_X = REG + 2
PATCH_Y = REG + 4
PATCH_Z = REG + 2


def patch_tables():
    inner = np.arange(1, CELLS + 1)
    x_side = axis_weights(np.concatenate([inner, [0, CELLS + 1]]), 0, PATCH_X)
    x_table = np.zeros((CELLS + 8, 16))
    x_table[: CELLS + 2, :PATCH_X] = x_side
    y_cells = np.arange(1 - EDGE, CELLS + EDGE + 1)
    y_side = axis_weights(y_cells, -1, PATCH_Y)
    y_out = axis_weights(np.array([-EDGE, CELLS + EDGE + 1]), -1, PATCH_Y)
    z_side = axis_weights(np.arange(CELLS + 2), 0, PATCH_Z)
    z_edge = np.zeros((CELLS, PATCH_Z))
    z_edge[0] = z_side[0]
    z_edge[-1] = z_side[-1]
    y_edge = np.zeros((LAYERS, PATCH_Y))
    y_edge[0] = y_out[0]
    y_edge[-1] = y_out[1]

    def both(ys, zs):
        return np.einsum("jb,kc->bcjk", ys, zs).reshape(PATCH_Y * PATCH_Z, WIDE)

    table = np.zeros((128, 3 * WIDE))
    table[: PATCH_Y * PATCH_Z] = np.concatenate(
        [both(y_side, z_side[1:-1]), both(y_side, z_edge), both(y_edge, z_side[1:-1])], axis=1
    )
    return x_table.astype(np.float32), table.astype(np.float32)


def from_behind(value, axis, steps):
    count = lax.axis_size(axis)
    initial, last = (max(0, -steps), min(count, count - steps))
    return lax.ppermute(value, axis, [(source, source + steps) for source in range(initial, last)])


def extended(block, axis, dim, width):
    count = lax.axis_size(axis)
    forward = [(i, (i + 1) % count) for i in range(count)]
    backward = [(target, source) for source, target in forward]
    low = lax.ppermute(
        lax.slice_in_dim(block, block.shape[dim] - width, None, axis=dim), axis, forward
    )
    high = lax.ppermute(lax.slice_in_dim(block, 0, width, axis=dim), axis, backward)
    return jnp.concatenate([low, block, high], axis=dim)


def decay(length, eig_first, eig_second):
    delta = -(eig_first + eig_second)
    delta = jnp.where(delta <= 0.0, 1.0, delta)
    q = 0.5 * delta + jnp.sqrt(delta + 0.25 * delta * delta)
    return 1.0 / (1.0 + q)


def moments_kernel(f_ref, eb_ref, ec_ref, out_ref):
    rows = f_ref.shape[0]
    r = decay(NR, eb_ref[...], ec_ref[...])
    up = f_ref[0]
    down = f_ref[rows - 1]
    for i in range(1, rows):
        up = r * up + f_ref[i]
        down = r * down + f_ref[rows - 1 - i]
    out_ref[0] = up
    out_ref[1] = down


def carry_kernel(rows, order, mom_ref, eb_ref, ec_ref, out_ref):
    blocks = mom_ref.shape[0]
    band = out_ref.shape[1] // 2
    r = decay(NR, eb_ref[...], ec_ref[...])
    ratio = r
    for _ in range(rows - 1):
        ratio = ratio * r
    total = jnp.ones_like(ratio)
    up = jnp.zeros_like(ratio)
    down = jnp.zeros_like(ratio)
    for k in range(blocks):
        total = total * ratio
        up = ratio * up + mom_ref[order[k], :band]
        down = ratio * down + mom_ref[order[blocks - 1 - k], band : 2 * band]
    norm = 1.0 / (1.0 - total)
    up = up * norm
    down = down * norm
    for k in range(blocks):
        out_ref[order[k], :band] = up
        up = ratio * up + mom_ref[order[k], :band]
        other = order[blocks - 1 - k]
        out_ref[other, band : 2 * band] = down
        down = ratio * down + mom_ref[other, band : 2 * band]


def solve_kernel(f_ref, carry_ref, eb_ref, ec_ref, zero_ref, out_ref):
    rows = f_ref.shape[0]
    r = decay(NR, eb_ref[...], ec_ref[...])
    scale = -r / ((1.0 - r) * (1.0 + r))
    tile = f_ref.shape[1]
    first = lax.broadcasted_iota(jnp.int32, r.shape, 0) + pl.program_id(0) * tile
    second = lax.broadcasted_iota(jnp.int32, r.shape, 1)
    zero_mode = (first == 0) & (second == 0)
    up = carry_ref[0]
    for i in range(rows):
        up = r * up + f_ref[i]
        out_ref[i] = up
    down = carry_ref[1]
    for i in range(rows - 1, -1, -1):
        down = r * down
        value = (out_ref[i] + down) * scale
        out_ref[i] = jnp.where(zero_mode, zero_ref[i][None, :], value)
        down = down + f_ref[i]


def subgrid_kernel(
    flag_ref, patch_ref, xt_ref, yz_ref, mid_ref, low_ref, high_ref, vel_ref, pot_ref, kick_ref
):
    slot = pl.program_id(0)
    live = flag_ref[0, slot] > 0
    has_below = flag_ref[1, slot] > 0
    has_above = flag_ref[2, slot] > 0
    back_below = flag_ref[3, slot] > 0
    back_above = flag_ref[4, slot] > 0
    planes = jnp.dot(patch_ref[0], yz_ref[...], precision=HIGHEST, preferred_element_type=F32)
    coarse = jnp.dot(xt_ref[...], planes, precision=HIGHEST, preferred_element_type=F32)
    start = coarse[:CELLS, :WIDE]
    x_low = coarse[CELLS : CELLS + 1, :WIDE]
    x_high = coarse[CELLS + 1 : CELLS + 2, :WIDE]
    z_edge = coarse[:CELLS, WIDE : 2 * WIDE]
    y_edge = coarse[:CELLS, 2 * WIDE :]
    shape = (CELLS, WIDE)
    row = lax.broadcasted_iota(jnp.int32, shape, 0)
    lane = lax.broadcasted_iota(jnp.int32, shape, 1)
    third = lane % CELLS
    side = EDGE * CELLS
    end = WIDE - side
    y_above = jnp.where(lane >= WIDE - CELLS, y_edge, pltpu.roll(start, WIDE - CELLS, 1))
    y_below = jnp.where(lane < CELLS, y_edge, pltpu.roll(start, CELLS, 1))
    cut_above = (lane >= WIDE - CELLS) | (
        (lane >= side - CELLS) & (lane < side) & jnp.logical_not(back_below)
    )
    cut_below = (lane < CELLS) | (
        (lane >= end) & (lane < end + CELLS) & jnp.logical_not(back_above)
    )
    fixed = ((lane < side) & jnp.logical_not(has_below)) | (
        (lane >= end) & jnp.logical_not(has_above)
    )
    rho = jnp.concatenate([low_ref[0], mid_ref[0], high_ref[0]], axis=1) * (1.0 / (REF * REF))

    def beside(v):
        return (
            (
                jnp.where(row == 0, x_low, pltpu.roll(v, 1, 0)),
                jnp.where(row == CELLS - 1, x_high, pltpu.roll(v, CELLS - 1, 0)),
            ),
            (
                jnp.where(cut_below, y_below, pltpu.roll(v, CELLS, 1)),
                jnp.where(cut_above, y_above, pltpu.roll(v, WIDE - CELLS, 1)),
            ),
            (
                jnp.where(third == 0, z_edge, pltpu.roll(v, 1, 1)),
                jnp.where(third == CELLS - 1, z_edge, pltpu.roll(v, WIDE - 1, 1)),
            ),
        )

    v = start
    for _ in range(SWEEPS):
        first, second, last = beside(v)
        total = first[1] + first[0] + second[1] + second[0] + last[1] + last[0]
        new = (1.0 - RELAXATION) * v + RELAXATION * (total - rho) / 6.0
        v = jnp.where(fixed, v, new)
    pot_ref[0] = jnp.where(live, v[:, side:end], 0.0)
    for q, (below, above) in enumerate(beside(v)):
        slope = (above[:, side:end] - below[:, side:end]) * (REF / 2.0)
        kick_ref[q, 0] = jnp.where(live, vel_ref[q, 0] - slope, 0.0)


def poisson(root_density, beside_work):
    size_first = lax.axis_size("px")
    size_second = lax.axis_size("py")
    devices = size_first * size_second
    device = lax.axis_index("px") * size_second + lax.axis_index("py")
    block = lax.axis_index("py") * size_first + lax.axis_index("px")
    order = [(k % size_first) * size_second + k // size_first for k in range(devices)]
    basis = jnp.asarray(fourier_basis(NR), F32)
    eig = -4.0 * np.sin(np.pi / NR * np.arange(NR)) ** 2
    eig_first = jnp.asarray(eig[:, None], F32)
    eig_second = jnp.asarray(eig[None, :], F32)
    rows = NR // devices
    band = NR // devices
    planes = lax.all_to_all(
        jnp.transpose(root_density, (1, 0, 2)), "px", split_axis=0, concat_axis=1, tiled=True
    )
    f = jnp.einsum("yxz,cz->yxc", planes, basis, precision=HIGH)
    f = jnp.einsum("yxc,ax->yac", f, basis, precision=HIGH)
    f, beside = lax.optimization_barrier((f, beside_work[0]))
    beside = beside_work[1](*beside)
    tile = 48
    grid = NR // tile
    f_spec = pl.BlockSpec((rows, tile, NR), lambda t: (0, t, 0))
    pair_spec = pl.BlockSpec((2, tile, NR), lambda t: (0, t, 0))
    eb_spec = pl.BlockSpec((tile, 1), lambda t: (t, 0))
    ec_spec = pl.BlockSpec((1, NR), lambda t: (0, 0))
    params = pltpu.CompilerParams(
        dimension_semantics=("arbitrary",), vmem_limit_bytes=60 * 1024 * 1024
    )
    moments = pl.pallas_call(
        moments_kernel,
        grid=(grid,),
        in_specs=[f_spec, eb_spec, ec_spec],
        out_specs=pair_spec,
        out_shape=jax.ShapeDtypeStruct((2, NR, NR), F32),
        compiler_params=params,
    )(f, eig_first, eig_second)
    column = jnp.pad(f[:, 0, 0], (0, NR - rows))
    sent = jnp.concatenate(
        [
            moments.reshape(2, devices, band, NR).transpose(1, 0, 2, 3).reshape(
                devices, 2 * band, NR
            ),
            jnp.broadcast_to(column[None, None, :], (devices, 8, NR)),
        ],
        axis=1,
    )
    got = lax.all_to_all(sent, ("px", "py"), split_axis=0, concat_axis=0, tiled=True)
    carries = pl.pallas_call(
        lambda *refs: carry_kernel(rows, order, *refs),
        out_shape=jax.ShapeDtypeStruct((devices, 2 * band, NR), F32),
        compiler_params=pltpu.CompilerParams(vmem_limit_bytes=60 * 1024 * 1024),
    )(got, lax.dynamic_slice_in_dim(eig_first, device * band, band, 0), eig_second)
    back = lax.all_to_all(carries, ("px", "py"), split_axis=0, concat_axis=0, tiled=True)
    back = back.reshape(devices, 2, band, NR).transpose(1, 0, 2, 3).reshape(2, NR, NR)
    back, beside = lax.optimization_barrier((back, beside))
    whole_column = got[:, 2 * band, :rows].reshape(size_first, size_second, rows)
    whole_column = whole_column.transpose(1, 0, 2).reshape(NR)
    own = lax.dynamic_slice_in_dim(
        jnp.asarray(pseudo_inverse(NR), F32), block * rows, rows, 0
    )
    zero_values = jnp.sum(own * whole_column[None, :], axis=1)
    zero_wide = jnp.broadcast_to(zero_values[:, None], (rows, NR))
    u = pl.pallas_call(
        solve_kernel,
        grid=(grid,),
        in_specs=[f_spec, pair_spec, eb_spec, ec_spec, pl.BlockSpec((rows, NR), lambda t: (0, 0))],
        out_specs=f_spec,
        out_shape=jax.ShapeDtypeStruct((rows, NR, NR), F32),
        compiler_params=params,
    )(f, back, eig_first, eig_second, zero_wide)
    u = jnp.einsum("yac,ax->yxc", u, basis, precision=HIGH)
    u = jnp.einsum("yxc,cz->yxz", u, basis, precision=HIGH)
    u = u.reshape(rows, size_first, NR // size_first, NR).transpose(1, 0, 2, 3)
    u = lax.all_to_all(u, "px", split_axis=0, concat_axis=0, tiled=True)
    return u.reshape(size_first * rows, NR // size_first, NR), beside


def local(root_density, subgrid_density, velocity, slot_anchor, slot_count, neighbour):
    first_rows, second_rows = root_density.shape[:2]
    size_second = lax.axis_size("py")
    place_first = lax.axis_index("px")
    place_second = lax.axis_index("py")
    device = place_first * size_second + place_second
    per_device = subgrid_density.shape[0]
    side = EDGE * CELLS
    inner = CELLS * CELLS
    positions = jnp.arange(per_device, dtype=jnp.int32)

    def early(density, anchors, counts, near):
        low_density = from_behind(density[:, :, inner - side :], "py", 1)
        high_density = from_behind(density[:, :, :side], "py", -1)
        owner = place_first * size_second + jnp.arange(size_second, dtype=jnp.int32)
        wanted = (place_second - jnp.arange(size_second, dtype=jnp.int32)) % size_second
        anchor = anchors[:, owner * per_device + wanted]
        x = jnp.clip(anchor[0] - place_first * first_rows, 0, first_rows - REG)
        y = jnp.clip(anchor[1] - place_second * second_rows, 0, second_rows - REG)
        columns = (anchor[2][:, None] - 1 + jnp.arange(PATCH_Z, dtype=jnp.int32)) % NR
        pick = (jnp.arange(NR, dtype=jnp.int32)[None, :, None] == columns[:, None, :]).astype(F32)
        slots = device * per_device + positions
        below, above = near[0][slots], near[1][slots]
        flags = jnp.stack(
            [
                positions < counts[device],
                below >= 0,
                above >= 0,
                near[1][jnp.maximum(below, 0)] >= 0,
                near[0][jnp.maximum(above, 0)] >= 0,
            ]
        ).astype(jnp.int32)
        return low_density, high_density, x, y, pick, flags

    held, (low_density, high_density, x, y, pick, flags) = poisson(
        root_density, ((subgrid_density, slot_anchor, slot_count, neighbour), early)
    )
    coarse_potential = jnp.transpose(held, (1, 0, 2))
    padded = extended(extended(held, "px", 1, 1), "py", 0, 2)
    cuts = jnp.stack(
        [
            lax.dynamic_slice(padded, (y[t], x[t], 0), (PATCH_Y, PATCH_X, NR))
            for t in range(size_second)
        ]
    )
    patches = jnp.einsum("tyxn,tnz->txyz", cuts, pick, precision=HIGHEST)
    patches = patches.reshape(size_second, -1)
    arrived = lax.all_to_all(
        patches, "py", split_axis=0, concat_axis=0, tiled=True
    )
    patch = arrived[(place_second + positions) % size_second]
    patch = patch.reshape(per_device, PATCH_X, PATCH_Y * PATCH_Z)
    patch = jnp.pad(
        patch, ((0, 0), (0, 16 - PATCH_X), (0, 128 - PATCH_Y * PATCH_Z))
    )
    x_table, yz_table = patch_tables()
    slot_spec = lambda width: pl.BlockSpec((1, CELLS, width), lambda s: (s, 0, 0))
    vel_spec = pl.BlockSpec((3, 1, CELLS, inner), lambda s: (0, s, 0, 0))
    potential, kicked = pl.pallas_call(
        subgrid_kernel,
        grid=(per_device,),
        in_specs=[
            pl.BlockSpec(memory_space=pltpu.SMEM),
            pl.BlockSpec((1, 16, 128), lambda s: (s, 0, 0)),
            pl.BlockSpec(x_table.shape, lambda s: (0, 0)),
            pl.BlockSpec(yz_table.shape, lambda s: (0, 0)),
            slot_spec(inner),
            slot_spec(side),
            slot_spec(side),
            vel_spec,
        ],
        out_specs=[slot_spec(inner), vel_spec],
        out_shape=[
            jax.ShapeDtypeStruct(subgrid_density.shape, F32),
            jax.ShapeDtypeStruct(velocity.shape, F32),
        ],
        compiler_params=pltpu.CompilerParams(
            dimension_semantics=("arbitrary",), vmem_limit_bytes=60 * 1024 * 1024
        ),
    )(
        flags,
        patch,
        jnp.asarray(x_table),
        jnp.asarray(yz_table),
        subgrid_density,
        low_density,
        high_density,
        velocity,
    )
    return (coarse_potential, potential, kicked)


def solution(mesh):
    return jax.shard_map(
        local,
        mesh=mesh,
        in_specs=(
            P("px", "py", None),
            P(("px", "py"), None, None),
            P(None, ("px", "py"), None, None),
            P(),
            P(),
            P(),
        ),
        out_specs=(
            P("px", "py", None),
            P(("px", "py"), None, None),
            P(None, ("px", "py"), None, None),
        ),
        check_vma=False,
    )
```
